32 devices in a mesh: date: 2 (over y), row: 16 (over z, x, core).
Axes of the slice: x: 2, y: 2, z: 4, core: 2. Of those that a mesh axis runs over, the one named last changes fastest.
Arguments:
- slc: float32 [2, 128, 128, 256], P(None, 'date', 'row'), may hold values from -40 to 40, as said below
- network: int32 [128, 8], replicated, may hold values 0 or 1
Outputs:
- linked: float32 [2, 128, 128, 256], P(None, None, 'row', 'date')
The draws below stay inside these ranges and needn't reach their ends.
Inputs may be any that keep to these rules, and one draw needn't show every extreme that they name: slc holds real and imaginary parts of complex samples.
All inputs are finite; a program needn't handle non-finite values.
Results may differ from the reference program's by a relative error of at most 0.0003.
Values sent between devices are 32-bit elements; how exact they have to be, the bound alone decides.
A program may use at most 192 MiB of HBM per device.

```python
import math
import jax
import jax.numpy as jnp
from jax import lax

DATES = 128
BAND = 8
LOOK = 5
ITERS = 5
ROW_DEV = 8
ROWS = 128
COLS = 256
N_ROW = 16


def draw_slc(key, part):
    keys = jax.random.split(key, 4)
    shape = (2, DATES, ROWS, COLS)
    noise = jax.random.truncated_normal(keys[0], -6.0, 6.0, shape, jnp.float32)
    amplitude = jnp.exp(jax.random.uniform(keys[1], (DATES, ROWS, COLS), jnp.float32, math.log(0.3), math.log(3.0)))
    common = 0.5
    shared = jax.random.truncated_normal(keys[2], -6.0, 6.0, (ROWS, COLS), jnp.float32)
    phases = jax.random.uniform(keys[3], (DATES,), jnp.float32, -math.pi, math.pi)
    part_re = amplitude * (noise[0] + common * shared[None] * jnp.cos(phases)[:, None, None])
    part_im = amplitude * (noise[1] + common * shared[None] * jnp.sin(phases)[:, None, None])
    return jnp.stack([part_re, part_im]).astype(jnp.float32)


def set_ends(drawn, own_key, smallest, largest):
    index_at = [jax.random.randint(jax.random.fold_in(own_key, axis), (), 0, length) for axis, length in enumerate(drawn.shape)]
    longest = drawn.shape.index(max(drawn.shape))
    next_to = index_at[:longest] + [(index_at[longest] + 1) % drawn.shape[longest]] + index_at[longest + 1:]
    return drawn.at[tuple(index_at)].set(smallest).at[tuple(next_to)].set(largest)


def setup_inputs(seed: int = 0) -> dict:
    seeds = jax.random.split(jax.random.key(seed), 3)
    slc = draw_slc(jax.random.fold_in(seeds[2], 71), 0)
    network = set_ends((jax.random.randint(seeds[1], (DATES, BAND), 0, 4) < 3).astype(jnp.int32), jax.random.fold_in(seeds[1], 1), 0, 1)
    return {"slc": slc, "network": network}


def band_table(count_out):
    count_in = count_out + 2 * LOOK
    outer = jnp.arange(count_out, dtype=jnp.int32)[:, None]
    inner = jnp.arange(count_in, dtype=jnp.int32)[None, :]
    reach = inner - outer
    return ((reach >= 0) & (reach <= 2 * LOOK)).astype(jnp.float32)

def box_sum(samples):
    rows_out = samples.shape[-2] - 2 * LOOK
    cols_out = samples.shape[-1] - 2 * LOOK
    row_table = band_table(rows_out)
    col_table = band_table(cols_out)
    total = jnp.einsum('...rc,kr->...kc', samples, row_table, precision=lax.Precision.HIGHEST)
    return jnp.einsum('...kc,mc->...km', total, col_table, precision=lax.Precision.HIGHEST)

def coherence(extended, network):
    num_dates = extended.shape[1]
    squares = extended[0] * extended[0] + extended[1] * extended[1]
    inverse_root = lax.rsqrt(box_sum(squares) + 1e-06)
    layers = []
    for offset in range(1, network.shape[1] + 1):
        earlier = extended[:, :num_dates - offset]
        later = extended[:, offset:]
        prod_re = earlier[0] * later[0] + earlier[1] * later[1]
        prod_im = earlier[1] * later[0] - earlier[0] * later[1]
        sums = box_sum(jnp.stack([prod_re, prod_im]))
        weight = network[:num_dates - offset, offset - 1].astype(jnp.float32)[:, None, None]
        weight = weight * inverse_root[:num_dates - offset] * inverse_root[offset:]
        layer = sums * weight[None]
        layers.append(jnp.pad(layer, ((0, 0), (0, offset), (0, 0), (0, 0))))
    return jnp.stack(layers)

def apply_matrix(coherent, vector):
    num_dates = vector.shape[1]
    image_re = vector[0]
    image_im = vector[1]
    for offset in range(1, coherent.shape[0] + 1):
        coh_re = coherent[offset - 1, 0]
        coh_im = coherent[offset - 1, 1]
        ahead = jnp.pad(vector[:, offset:], ((0, 0), (0, offset), (0, 0), (0, 0)))
        image_re = image_re + coh_re * ahead[0] - coh_im * ahead[1]
        image_im = image_im + coh_re * ahead[1] + coh_im * ahead[0]
        back_re = coh_re * vector[0] + coh_im * vector[1]
        back_im = coh_re * vector[1] - coh_im * vector[0]
        image_re = image_re + jnp.pad(back_re[:num_dates - offset], ((offset, 0), (0, 0), (0, 0)))
        image_im = image_im + jnp.pad(back_im[:num_dates - offset], ((offset, 0), (0, 0), (0, 0)))
    image = jnp.stack([image_re, image_im])
    meansq = lax.optimization_barrier(jnp.mean(image[0] * image[0] + image[1] * image[1], axis=0))
    return image * lax.rsqrt(meansq + 1e-06)[None, None]

def power_iterate(coherent):
    start = jnp.stack([jnp.ones_like(coherent[0, 0]), jnp.zeros_like(coherent[0, 0])])

    def iterate_once(index, vector):
        return apply_matrix(coherent, vector)
    return lax.fori_loop(0, ITERS, iterate_once, start)

def reference(slc, network):
    padded = jnp.pad(slc, ((0, 0), (0, 0), (LOOK, LOOK), (LOOK, LOOK)))

    def one_strip(strip):
        first = (strip * ROW_DEV).astype(jnp.int32)
        extended = lax.dynamic_slice_in_dim(padded, first, ROW_DEV + 2 * LOOK, 2)
        return power_iterate(coherence(extended, network))
    strips = lax.map(one_strip, jnp.arange(N_ROW, dtype=jnp.int32))
    strips = jnp.transpose(strips, (1, 2, 0, 3, 4))
    return strips.reshape(2, DATES, ROWS, COLS)
```

```python
import functools

import jax
import jax.numpy as jnp
from jax import lax
from jax.experimental import pallas as pl
from jax.experimental.pallas import tpu as pltpu
from jax.sharding import PartitionSpec as P

LOOK = 5
ITERS = 5
SUB = 8
MESH = pl.DeviceIdType.MESH


def pack_kernel(nd, x_ref, s_ref):
    _, dates, rows, cols = x_ref.shape
    width = cols // nd
    groups = dates // SUB
    slot = width // groups
    lane = lax.broadcasted_iota(jnp.int32, (rows, SUB, width), 2)
    for comp in range(2):
        rims = [jnp.zeros((rows, SUB, width), jnp.float32) for _ in range(nd)]
        for g in range(groups):
            near = pl.ds(g * SUB, SUB)
            tiles = []
            for c in range(nd):
                tile = x_ref[comp, near, :, pl.ds(c * width, width)]
                tile = jnp.transpose(tile, (1, 0, 2))
                s_ref[c, comp, :, near, :] = tile
                tiles.append(tile)
            first = slot * g
            for c in range(nd):
                if c > 0:
                    moved = pltpu.roll(tiles[c - 1], (first + LOOK) % width, 2)
                    rims[c] = jnp.where((lane >= first) & (lane < first + LOOK), moved, rims[c])
                if c < nd - 1:
                    moved = pltpu.roll(tiles[c + 1], (first + LOOK) % width, 2)
                    rims[c] = jnp.where((lane >= first + LOOK) & (lane < first + 2 * LOOK), moved, rims[c])
        for c in range(nd):
            s_ref[c, comp, :, pl.ds(dates, SUB), :] = rims[c]


def send_kernel(nd, nr, s_ref, e_ref, give_sem, take_sem, up_send, up_recv, down_send, down_recv):
    rows = s_ref.shape[2]
    me = lax.axis_index("date")
    row = lax.axis_index("row")
    has_up = row > 0
    has_down = row < nr - 1
    up = jnp.maximum(row - 1, 0)
    down = jnp.minimum(row + 1, nr - 1)
    barrier = pltpu.get_barrier_semaphore()
    for k in range(1, nd):
        pl.semaphore_signal(barrier, 1, device_id=(lax.rem(me + k, nd), row), device_id_type=MESH)

    @pl.when(has_up)
    def _():
        pl.semaphore_signal(barrier, 1, device_id=(me, up), device_id_type=MESH)

    @pl.when(has_down)
    def _():
        pl.semaphore_signal(barrier, 1, device_id=(me, down), device_id_type=MESH)

    pl.semaphore_wait(barrier, nd - 1 + has_up.astype(jnp.int32) + has_down.astype(jnp.int32))

    def give(k, comp):
        there = lax.rem(me + k, nd)
        return pltpu.make_async_remote_copy(
            src_ref=s_ref.at[there, comp],
            dst_ref=e_ref.at[me, comp, pl.ds(LOOK, rows)],
            send_sem=give_sem.at[k, comp],
            recv_sem=take_sem.at[k, comp],
            device_id=(there, row),
            device_id_type=MESH,
        )

    def rim(k, comp, to_up):
        source = lax.rem(me + nd - k, nd)
        begin = 0 if to_up else rows - LOOK
        if k == 0:
            src = s_ref.at[me, comp, pl.ds(begin, LOOK)]
        else:
            src = e_ref.at[source, comp, pl.ds(LOOK + begin, LOOK)]
        return pltpu.make_async_remote_copy(
            src_ref=src,
            dst_ref=e_ref.at[source, comp, pl.ds(LOOK + rows if to_up else 0, LOOK)],
            send_sem=(up_send if to_up else down_send).at[k, comp],
            recv_sem=(up_recv if to_up else down_recv).at[k, comp],
            device_id=(me, up if to_up else down),
            device_id_type=MESH,
        )

    def start_rims(k, comp):
        @pl.when(has_up)
        def _():
            rim(k, comp, True).start()

        @pl.when(has_down)
        def _():
            rim(k, comp, False).start()

    for comp in range(2):
        for k in range(1, nd):
            give(k, comp).start()
        start_rims(0, comp)
    for comp in range(2):
        for k in range(1, nd):
            give(k, comp).wait_recv()
            start_rims(k, comp)
    for comp in range(2):
        for k in range(1, nd):
            give(k, comp).wait_send()
    for comp in range(2):
        for k in range(nd):

            @pl.when(has_up)
            def _():
                rim(k, comp, True).wait_send()
                rim(k, comp, False).wait_recv()

            @pl.when(has_down)
            def _():
                rim(k, comp, False).wait_send()
                rim(k, comp, True).wait_recv()


def row_sums(cells):
    span = 2 * LOOK + 1
    count = len(cells) - span + 1
    head = functools.reduce(jnp.add, cells[count - 1 : span])
    heads = [head]
    for k in range(count - 2, -1, -1):
        heads.append(heads[-1] + cells[k])
    heads = heads[::-1]
    sums = [heads[0]]
    tail = None
    for k in range(1, count):
        cell = cells[span + k - 1]
        tail = cell if tail is None else tail + cell
        sums.append(heads[k] + tail)
    return sums


def halves(sums):
    stacked = jnp.concatenate(sums, axis=0)
    high = stacked.astype(jnp.bfloat16)
    low = (stacked - high.astype(jnp.float32)).astype(jnp.bfloat16)
    return high, low


def products(load, offset):
    depth = load.rows
    if offset == 0:
        squares = []
        for r in range(depth):
            re, im = load(0, r, 0), load(1, r, 0)
            squares.append(re * re + im * im)
        return row_sums(squares)
    part_re, part_im = [], []
    for r in range(depth):
        a_re, a_im = load(0, r, 0), load(1, r, 0)
        b_re, b_im = load(0, r, offset), load(1, r, offset)
        part_re.append(a_re * b_re + a_im * b_im)
        part_im.append(a_im * b_re - a_re * b_im)
    return row_sums(part_re) + row_sums(part_im)


class Loader:
    def __init__(self, read, rows):
        self.read = read
        self.rows = rows

    def __call__(self, comp, row, offset):
        return self.read(comp, row, offset)


def link_kernel(nd, nr, s_ref, e_ref, net_ref, out_ref, main, rim, rim_high, rim_low, table, root, gam, vec):
    rows, width = out_ref.shape[2], out_ref.shape[3]
    dates = out_ref.shape[1]
    band = net_ref.shape[1]
    local = dates // nd
    groups = local // SUB
    slot = width // groups
    tiles = dates // SUB
    tall = rows + 2 * LOOK
    me = lax.axis_index("date")
    row = lax.axis_index("row")
    has_up = row > 0
    has_down = row < nr - 1

    lane = lax.broadcasted_iota(jnp.int32, (SUB, width), 1)
    for comp in range(2):
        for r in range(tall):
            inner = LOOK <= r < LOOK + rows
            keep = None if inner else (has_up if r < LOOK else has_down)
            for s in range(nd):
                block = e_ref[s, comp, r, pl.ds(0, local), :]
                edge = e_ref[s, comp, r, pl.ds(local, SUB), :]
                if keep is not None:
                    block = jnp.where(keep, block, 0.0)
                    edge = jnp.where(keep, edge, 0.0)
                main[comp, r, pl.ds(s * local, local), :] = block
                rim[s, comp, r, pl.ds(0, SUB), :] = edge
            if inner:
                main[comp, r, pl.ds(pl.multiple_of(me * local, SUB), local), :] = s_ref[me, comp, r - LOOK, pl.ds(0, local), :]
                rim[me, comp, r, pl.ds(0, SUB), :] = s_ref[me, comp, r - LOOK, pl.ds(local, SUB), :]
            main[comp, r, pl.ds(dates, SUB), :] = jnp.zeros((SUB, width), jnp.float32)
            for s in range(nd):
                later = pltpu.roll(rim[s, comp, r, pl.ds(0, SUB), :], width - slot, 1)
                if s + 1 < nd:
                    last = pltpu.roll(rim[s + 1, comp, r, pl.ds(0, SUB), :], slot * (groups - 1), 1)
                else:
                    last = jnp.zeros((SUB, width), jnp.float32)
                rim[s, comp, r, pl.ds(SUB, SUB), :] = jnp.where(lane >= slot * (groups - 1), last, later)

    inner = lax.broadcasted_iota(jnp.int32, (width, width), 0)
    outer = lax.broadcasted_iota(jnp.int32, (width, width), 1)
    for g in range(groups):
        table[g, pl.ds(0, width), :] = (jnp.abs(inner - outer) <= LOOK).astype(jnp.float32).astype(jnp.bfloat16)
        cell = inner - slot * g
        left = (cell >= 0) & (cell < LOOK) & (outer <= cell)
        right = (cell >= LOOK) & (cell < 2 * LOOK) & (outer >= width + cell - 2 * LOOK)
        table[g, pl.ds(width, width), :] = (left | right).astype(jnp.float32).astype(jnp.bfloat16)

    def rim_sums(s, carry):
        load = Loader(lambda comp, r, off: rim[s, comp, r, pl.ds(off, SUB), :], tall)
        begin = 0
        for offset in range(band + 1):
            high, low = halves(products(load, offset))
            rim_high[s, pl.ds(begin, high.shape[0]), :] = high
            rim_low[s, pl.ds(begin, high.shape[0]), :] = low
            begin += high.shape[0]
        return carry

    lax.fori_loop(0, nd, rim_sums, 0)

    for k in range(rows):
        root[k, pl.ds(dates, SUB), :] = jnp.zeros((SUB, width), jnp.float32)

    def tile_sums(index, carry):
        t = tiles - 1 - index
        s, g = t // groups, lax.rem(t, groups)
        base = t * SUB
        load = Loader(lambda comp, r, off: main[comp, r, pl.ds(base + off, SUB), :], tall)
        used = net_ref[pl.ds(base, SUB), :].astype(jnp.float32)
        begin = 0
        for offset in range(band + 1):
            high, low = halves(products(load, offset))
            count = high.shape[0]
            high = jnp.concatenate([high, rim_high[s, pl.ds(begin, count), :]], axis=1)
            low = jnp.concatenate([low, rim_low[s, pl.ds(begin, count), :]], axis=1)
            begin += count
            sums = jnp.dot(jnp.concatenate([high, low], axis=0), table[g], preferred_element_type=jnp.float32)
            sums = sums[:count] + sums[count:]
            for k in range(rows):
                if offset == 0:
                    root[k, pl.ds(base, SUB), :] = lax.rsqrt(sums[k * SUB : (k + 1) * SUB] + 1e-06)
                else:
                    weight = root[k, pl.ds(base, SUB), :] * root[k, pl.ds(base + offset, SUB), :]
                    weight = weight * used[:, offset - 1 : offset]
                    at = pl.ds(base * rows + k, SUB, stride=rows)
                    gam[0, offset - 1, at, :] = sums[k * SUB : (k + 1) * SUB] * weight
                    gam[1, offset - 1, at, :] = sums[(rows + k) * SUB : (rows + k + 1) * SUB] * weight
        return carry

    lax.fori_loop(0, tiles, tile_sums, 0)

    zero = jnp.zeros((rows, width), jnp.float32)
    for buf in range(2):
        for comp in range(2):
            for d in range(band):
                vec[buf, comp, dates + d] = zero

    def fill(d, carry):
        vec[0, 0, d] = zero + 1.0
        vec[0, 1, d] = zero
        return carry

    lax.fori_loop(0, dates, fill, 0)

    def iterate(step, scale):
        now = lax.rem(step, 2)
        after = 1 - now

        def block(b, carry):
            acc, near, total = carry
            acc_re, acc_im = [list(a) for a in acc]
            v_re, v_im = [list(a) for a in near]
            for j in range(SUB):
                d = b * SUB + j
                v_re.append(vec[now, 0, d + band])
                v_im.append(vec[now, 1, d + band])
                y_re = acc_re[j] + v_re[j]
                y_im = acc_im[j] + v_im[j]
                at = pl.ds(pl.multiple_of(d * rows, rows), rows)
                for o in range(1, band + 1):
                    c_re = gam[0, o - 1, at, :]
                    c_im = gam[1, o - 1, at, :]
                    y_re = y_re + (c_re * v_re[j + o] - c_im * v_im[j + o])
                    y_im = y_im + (c_re * v_im[j + o] + c_im * v_re[j + o])
                    back_re = c_re * v_re[j] + c_im * v_im[j]
                    back_im = c_re * v_im[j] - c_im * v_re[j]
                    if o == band:
                        acc_re.append(back_re)
                        acc_im.append(back_im)
                    else:
                        acc_re[j + o] = acc_re[j + o] + back_re
                        acc_im[j + o] = acc_im[j + o] + back_im
                vec[after, 0, d] = y_re
                vec[after, 1, d] = y_im
                total = total + (y_re * y_re + y_im * y_im)
            acc = tuple(acc_re[SUB:]), tuple(acc_im[SUB:])
            near = tuple(v_re[SUB:]), tuple(v_im[SUB:])
            return acc, near, total

        none = tuple(zero for _ in range(band))
        near = tuple(tuple(vec[now, comp, d] for d in range(band)) for comp in range(2))
        _, _, total = lax.fori_loop(0, tiles, block, ((none, none), near, zero))
        return scale * lax.rsqrt(scale * scale * (total / dates) + 1e-06)

    scale = lax.fori_loop(0, ITERS, iterate, zero + 1.0)
    final = ITERS % 2

    def finish(d, carry):
        out_ref[0, d] = vec[final, 0, d] * scale
        out_ref[1, d] = vec[final, 1, d] * scale
        return carry

    lax.fori_loop(0, dates, finish, 0)


def on_device(nd, nr, slc, network):
    _, local, rows, cols = slc.shape
    width = cols // nd
    dates, band = network.shape
    tall = rows + 2 * LOOK
    maps = (2 * band + 1) * rows * SUB
    whole = pl.BlockSpec(memory_space=pltpu.VMEM)
    away = pl.BlockSpec(memory_space=pl.ANY)
    packed = pl.pallas_call(
        functools.partial(pack_kernel, nd),
        out_shape=jax.ShapeDtypeStruct((nd, 2, rows, local + SUB, width), jnp.float32),
        in_specs=[whole],
        out_specs=whole,
        name="pack",
    )(slc)
    sems = pltpu.SemaphoreType.DMA((nd, 2))
    landed = pl.pallas_call(
        functools.partial(send_kernel, nd, nr),
        out_shape=jax.ShapeDtypeStruct((nd, 2, tall, local + SUB, width), jnp.float32),
        in_specs=[away],
        out_specs=away,
        scratch_shapes=[sems] * 6,
        compiler_params=pltpu.CompilerParams(collective_id=0, has_side_effects=True),
        name="send",
    )(packed)
    return pl.pallas_call(
        functools.partial(link_kernel, nd, nr),
        out_shape=jax.ShapeDtypeStruct((2, dates, rows, width), jnp.float32),
        in_specs=[whole] * 3,
        out_specs=whole,
        scratch_shapes=[
            pltpu.VMEM((2, tall, dates + SUB, width), jnp.float32),
            pltpu.VMEM((nd, 2, tall, 2 * SUB, width), jnp.float32),
            pltpu.VMEM((nd, maps, width), jnp.bfloat16),
            pltpu.VMEM((nd, maps, width), jnp.bfloat16),
            pltpu.VMEM((local // SUB, 2 * width, width), jnp.bfloat16),
            pltpu.VMEM((rows, dates + SUB, width), jnp.float32),
            pltpu.VMEM((2, band, dates * rows, width), jnp.float32),
            pltpu.VMEM((2, 2, dates + band, rows, width), jnp.float32),
        ],
        compiler_params=pltpu.CompilerParams(vmem_limit_bytes=48 * 1024 * 1024),
        name="link",
    )(packed, landed, network)


def solution(mesh):
    return jax.shard_map(
        functools.partial(on_device, mesh.shape["date"], mesh.shape["row"]),
        mesh=mesh,
        in_specs=(P(None, "date", "row", None), P()),
        out_specs=P(None, None, "row", "date"),
        check_vma=False,
    )
```

```python
import functools

import jax
import jax.numpy as jnp
from jax import lax
from jax.experimental import pallas as pl
from jax.experimental.pallas import tpu as pltpu
from jax.sharding import PartitionSpec as P

LOOK = 5
ITERS = 5
SUB = 8
STEP = 8
MESH = pl.DeviceIdType.MESH


def pack_kernel(nd, x_ref, s_ref):
    _, dates, rows, cols = x_ref.shape
    width = cols // nd
    groups = dates // SUB
    slot = width // groups
    lane = lax.broadcasted_iota(jnp.int32, (rows, SUB, width), 2)
    for comp in range(2):
        rims = [jnp.zeros((rows, SUB, width), jnp.float32) for _ in range(nd)]
        for g in range(groups):
            near = pl.ds(g * SUB, SUB)
            tiles = []
            for c in range(nd):
                tile = x_ref[comp, near, :, pl.ds(c * width, width)]
                tile = jnp.transpose(tile, (1, 0, 2))
                s_ref[c, comp, :, near, :] = tile
                tiles.append(tile)
            first = slot * g
            for c in range(nd):
                if c > 0:
                    moved = pltpu.roll(tiles[c - 1], (first + LOOK) % width, 2)
                    rims[c] = jnp.where((lane >= first) & (lane < first + LOOK), moved, rims[c])
                if c < nd - 1:
                    moved = pltpu.roll(tiles[c + 1], (first + LOOK) % width, 2)
                    rims[c] = jnp.where((lane >= first + LOOK) & (lane < first + 2 * LOOK), moved, rims[c])
        for c in range(nd):
            s_ref[c, comp, :, pl.ds(dates, SUB), :] = rims[c]


def send_kernel(nd, nr, s_ref, e_ref, give_sem, take_sem, up_send, up_recv, down_send, down_recv):
    rows, deep = s_ref.shape[2:4]
    parts = give_sem.shape[1] // 2
    piece = deep // parts
    chunks = [(comp, part) for comp in range(2) for part in range(parts)]
    me = lax.axis_index("date")
    row = lax.axis_index("row")
    has_up = row > 0
    has_down = row < nr - 1
    up = jnp.maximum(row - 1, 0)
    down = jnp.minimum(row + 1, nr - 1)
    barrier = pltpu.get_barrier_semaphore()
    for k in range(1, nd):
        pl.semaphore_signal(barrier, 1, device_id=(lax.rem(me + k, nd), row), device_id_type=MESH)

    @pl.when(has_up)
    def _():
        pl.semaphore_signal(barrier, 1, device_id=(me, up), device_id_type=MESH)

    @pl.when(has_down)
    def _():
        pl.semaphore_signal(barrier, 1, device_id=(me, down), device_id_type=MESH)

    pl.semaphore_wait(barrier, nd - 1 + has_up.astype(jnp.int32) + has_down.astype(jnp.int32))

    def give(k, n):
        comp, part = chunks[n]
        there = lax.rem(me + k, nd)
        near = pl.ds(part * piece, piece)
        return pltpu.make_async_remote_copy(
            src_ref=s_ref.at[there, comp, :, near],
            dst_ref=e_ref.at[me, comp, pl.ds(LOOK, rows), near],
            send_sem=give_sem.at[k, n],
            recv_sem=take_sem.at[k, n],
            device_id=(there, row),
            device_id_type=MESH,
        )

    def rim(k, n, to_up):
        comp, part = chunks[n]
        near = pl.ds(part * piece, piece)
        source = lax.rem(me + nd - k, nd)
        begin = 0 if to_up else rows - LOOK
        if k == 0:
            src = s_ref.at[me, comp, pl.ds(begin, LOOK), near]
        else:
            src = e_ref.at[source, comp, pl.ds(LOOK + begin, LOOK), near]
        return pltpu.make_async_remote_copy(
            src_ref=src,
            dst_ref=e_ref.at[source, comp, pl.ds(LOOK + rows if to_up else 0, LOOK), near],
            send_sem=(up_send if to_up else down_send).at[k, n],
            recv_sem=(up_recv if to_up else down_recv).at[k, n],
            device_id=(me, up if to_up else down),
            device_id_type=MESH,
        )

    def start_rims(k, n):
        @pl.when(has_up)
        def _():
            rim(k, n, True).start()

        @pl.when(has_down)
        def _():
            rim(k, n, False).start()

    for n in range(len(chunks)):
        for k in range(1, nd):
            give(k, n).start()
        start_rims(0, n)
    for n in range(len(chunks)):
        for k in range(1, nd):
            give(k, n).wait_recv()
            start_rims(k, n)
    for n in range(len(chunks)):
        for k in range(1, nd):
            give(k, n).wait_send()
    for n in range(len(chunks)):
        for k in range(nd):

            @pl.when(has_up)
            def _():
                rim(k, n, True).wait_send()
                rim(k, n, False).wait_recv()

            @pl.when(has_down)
            def _():
                rim(k, n, False).wait_send()
                rim(k, n, True).wait_recv()


def row_sums(cells):
    span = 2 * LOOK + 1
    count = len(cells) - span + 1
    head = functools.reduce(jnp.add, cells[count - 1 : span])
    heads = [head]
    for k in range(count - 2, -1, -1):
        heads.append(heads[-1] + cells[k])
    heads = heads[::-1]
    sums = [heads[0]]
    tail = None
    for k in range(1, count):
        cell = cells[span + k - 1]
        tail = cell if tail is None else tail + cell
        sums.append(heads[k] + tail)
    return sums


def halves(sums):
    stacked = jnp.concatenate(sums, axis=0)
    high = stacked.astype(jnp.bfloat16)
    low = (stacked - high.astype(jnp.float32)).astype(jnp.bfloat16)
    return high, low


def products(load, offset):
    depth = load.rows
    if offset == 0:
        squares = []
        for r in range(depth):
            re, im = load(0, r, 0), load(1, r, 0)
            squares.append(re * re + im * im)
        return row_sums(squares)
    part_re, part_im = [], []
    for r in range(depth):
        a_re, a_im = load(0, r, 0), load(1, r, 0)
        b_re, b_im = load(0, r, offset), load(1, r, offset)
        part_re.append(a_re * b_re + a_im * b_im)
        part_im.append(a_im * b_re - a_re * b_im)
    return row_sums(part_re) + row_sums(part_im)


class Loader:
    def __init__(self, read, rows):
        self.read = read
        self.rows = rows

    def __call__(self, comp, row, offset):
        return self.read(comp, row, offset)


def link_kernel(nd, nr, s_ref, e_ref, net_ref, out_ref, main, rim, rim_high, rim_low, table, root, gam, vec, used_at):
    rows, width = out_ref.shape[2], out_ref.shape[3]
    dates = out_ref.shape[1]
    band = net_ref.shape[0]
    local = dates // nd
    groups = local // SUB
    slot = width // groups
    tiles = dates // SUB
    tall = rows + 2 * LOOK
    me = lax.axis_index("date")
    row = lax.axis_index("row")
    has_up = row > 0
    has_down = row < nr - 1

    used_at[...] = jnp.transpose(net_ref[...].astype(jnp.float32), (1, 0))

    lane = lax.broadcasted_iota(jnp.int32, (SUB, width), 1)
    for comp in range(2):
        for r in range(tall):
            inner = LOOK <= r < LOOK + rows
            keep = None if inner else (has_up if r < LOOK else has_down)
            for s in range(nd):
                block = e_ref[s, comp, r, pl.ds(0, local), :]
                edge = e_ref[s, comp, r, pl.ds(local, SUB), :]
                if keep is not None:
                    block = jnp.where(keep, block, 0.0)
                    edge = jnp.where(keep, edge, 0.0)
                main[comp, r, pl.ds(s * local, local), :] = block
                rim[s, comp, r, pl.ds(0, SUB), :] = edge
            if inner:
                main[comp, r, pl.ds(pl.multiple_of(me * local, SUB), local), :] = s_ref[me, comp, r - LOOK, pl.ds(0, local), :]
                rim[me, comp, r, pl.ds(0, SUB), :] = s_ref[me, comp, r - LOOK, pl.ds(local, SUB), :]
            main[comp, r, pl.ds(dates, SUB), :] = jnp.zeros((SUB, width), jnp.float32)
            for s in range(nd):
                later = pltpu.roll(rim[s, comp, r, pl.ds(0, SUB), :], width - slot, 1)
                if s + 1 < nd:
                    last = pltpu.roll(rim[s + 1, comp, r, pl.ds(0, SUB), :], slot * (groups - 1), 1)
                else:
                    last = jnp.zeros((SUB, width), jnp.float32)
                rim[s, comp, r, pl.ds(SUB, SUB), :] = jnp.where(lane >= slot * (groups - 1), last, later)

    inner = lax.broadcasted_iota(jnp.int32, (width, width), 0)
    outer = lax.broadcasted_iota(jnp.int32, (width, width), 1)
    for g in range(groups):
        table[g, pl.ds(0, width), :] = (jnp.abs(inner - outer) <= LOOK).astype(jnp.float32).astype(jnp.bfloat16)
        cell = inner - slot * g
        left = (cell >= 0) & (cell < LOOK) & (outer <= cell)
        right = (cell >= LOOK) & (cell < 2 * LOOK) & (outer >= width + cell - 2 * LOOK)
        table[g, pl.ds(width, width), :] = (left | right).astype(jnp.float32).astype(jnp.bfloat16)

    def rim_sums(s, carry):
        load = Loader(lambda comp, r, off: rim[s, comp, r, pl.ds(off, SUB), :], tall)
        begin = 0
        for offset in range(band + 1):
            high, low = halves(products(load, offset))
            rim_high[s, pl.ds(begin, high.shape[0]), :] = high
            rim_low[s, pl.ds(begin, high.shape[0]), :] = low
            begin += high.shape[0]
        return carry

    lax.fori_loop(0, nd, rim_sums, 0)

    for k in range(rows):
        root[k, pl.ds(dates, SUB), :] = jnp.zeros((SUB, width), jnp.float32)

    def tile_sums(index, carry):
        t = tiles - 1 - index
        s, g = t // groups, lax.rem(t, groups)
        base = t * SUB
        load = Loader(lambda comp, r, off: main[comp, r, pl.ds(base + off, SUB), :], tall)
        used = used_at[pl.ds(base, SUB), :]
        begin = 0
        for offset in range(band + 1):
            high, low = halves(products(load, offset))
            count = high.shape[0]
            high = jnp.concatenate([high, rim_high[s, pl.ds(begin, count), :]], axis=1)
            low = jnp.concatenate([low, rim_low[s, pl.ds(begin, count), :]], axis=1)
            begin += count
            sums = jnp.dot(jnp.concatenate([high, low], axis=0), table[g], preferred_element_type=jnp.float32)
            sums = sums[:count] + sums[count:]
            for k in range(rows):
                if offset == 0:
                    root[k, pl.ds(base, SUB), :] = lax.rsqrt(sums[k * SUB : (k + 1) * SUB] + 1e-06)
                else:
                    weight = root[k, pl.ds(base, SUB), :] * root[k, pl.ds(base + offset, SUB), :]
                    weight = weight * used[:, offset - 1 : offset]
                    at = pl.ds(base * rows + k, SUB, stride=rows)
                    c_re = sums[k * SUB : (k + 1) * SUB] * weight
                    c_im = sums[(rows + k) * SUB : (rows + k + 1) * SUB] * weight
                    gam[0, offset - 1, at, :] = c_re
                    gam[1, offset - 1, at, :] = c_re + c_im
                    gam[2, offset - 1, at, :] = c_im - c_re
        return carry

    lax.fori_loop(0, tiles, tile_sums, 0)

    zero = jnp.zeros((rows, width), jnp.float32)
    for buf in range(2):
        for comp in range(2):
            for d in range(band):
                vec[buf, comp, dates + d] = zero

    def at_date(d):
        return pl.ds(pl.multiple_of(d * rows, rows), rows)

    def first(b, carry):
        back_re, back_sum, total = list(carry[0]), list(carry[1]), carry[2]
        for j in range(SUB):
            d = b * SUB + j
            y_re = back_re[j] + 1.0
            y_im = back_re[j] - back_sum[j]
            ahead_re = ahead_sum = None
            for o in range(1, band + 1):
                c_re = gam[0, o - 1, at_date(d), :]
                c_sum = gam[1, o - 1, at_date(d), :]
                ahead_re = c_re if ahead_re is None else ahead_re + c_re
                ahead_sum = c_sum if ahead_sum is None else ahead_sum + c_sum
                if o == band:
                    back_re.append(c_re)
                    back_sum.append(c_sum)
                else:
                    back_re[j + o] = back_re[j + o] + c_re
                    back_sum[j + o] = back_sum[j + o] + c_sum
            y_re = y_re + ahead_re
            y_im = y_im + (ahead_sum - ahead_re)
            vec[1, 0, d] = y_re
            vec[1, 1, d] = y_im
            total = total + (y_re * y_re + y_im * y_im)
        return tuple(back_re[SUB:]), tuple(back_sum[SUB:]), total

    none = tuple(zero for _ in range(band))
    _, _, total = lax.fori_loop(0, tiles, first, (none, none, zero))
    scale = lax.rsqrt(total / dates + 1e-06)

    def iterate(step, scale):
        now = lax.rem(step, 2)
        after = 1 - now

        def block(b, carry):
            acc, near, total = carry
            acc_a, acc_b, acc_c = [list(a) for a in acc]
            v_re, v_im, v_sum = [list(a) for a in near]
            for j in range(STEP):
                d = b * STEP + j
                v_re.append(vec[now, 0, d + band])
                v_im.append(vec[now, 1, d + band])
                v_sum.append(v_re[-1] + v_im[-1])
                y_a, y_b, y_c = acc_a[j], -acc_b[j], -acc_c[j]
                for o in range(1, band + 1):
                    c_re = gam[0, o - 1, at_date(d), :]
                    c_sum = gam[1, o - 1, at_date(d), :]
                    c_dif = gam[2, o - 1, at_date(d), :]
                    y_a = y_a + c_re * v_sum[j + o]
                    y_b = y_b + c_dif * v_re[j + o]
                    y_c = y_c + c_sum * v_im[j + o]
                    back_a = c_re * v_sum[j]
                    back_b = c_sum * v_re[j]
                    back_c = c_dif * v_im[j]
                    if o == band:
                        acc_a.append(back_a)
                        acc_b.append(back_b)
                        acc_c.append(back_c)
                    else:
                        acc_a[j + o] = acc_a[j + o] + back_a
                        acc_b[j + o] = acc_b[j + o] + back_b
                        acc_c[j + o] = acc_c[j + o] + back_c
                y_re = v_re[j] + (y_a - y_c)
                y_im = v_im[j] + (y_a + y_b)
                vec[after, 0, d] = y_re
                vec[after, 1, d] = y_im
                total = total + (y_re * y_re + y_im * y_im)
            acc = tuple(acc_a[STEP:]), tuple(acc_b[STEP:]), tuple(acc_c[STEP:])
            near = tuple(v_re[STEP:]), tuple(v_im[STEP:]), tuple(v_sum[STEP:])
            return acc, near, total

        v_re = tuple(vec[now, 0, d] for d in range(band))
        v_im = tuple(vec[now, 1, d] for d in range(band))
        v_sum = tuple(a + b for a, b in zip(v_re, v_im))
        _, _, total = lax.fori_loop(0, dates // STEP, block, ((none, none, none), (v_re, v_im, v_sum), zero))
        return scale * lax.rsqrt(scale * scale * (total / dates) + 1e-06)

    scale = lax.fori_loop(1, ITERS, iterate, scale)
    final = ITERS % 2

    def finish(b, carry):
        for j in range(SUB):
            d = b * SUB + j
            out_ref[0, d] = vec[final, 0, d] * scale
            out_ref[1, d] = vec[final, 1, d] * scale
        return carry

    lax.fori_loop(0, tiles, finish, 0)


def on_device(nd, nr, slc, network):
    _, local, rows, cols = slc.shape
    width = cols // nd
    dates, band = network.shape
    tall = rows + 2 * LOOK
    maps = (2 * band + 1) * rows * SUB
    whole = pl.BlockSpec(memory_space=pltpu.VMEM)
    packed = pl.pallas_call(
        functools.partial(pack_kernel, nd),
        out_shape=jax.ShapeDtypeStruct((nd, 2, rows, local + SUB, width), jnp.float32),
        in_specs=[whole],
        out_specs=whole,
        name="pack",
    )(slc)
    parts = 3 if (local + SUB) % (3 * SUB) == 0 else 1
    sems = pltpu.SemaphoreType.DMA((nd, 2 * parts))
    landed = pl.pallas_call(
        functools.partial(send_kernel, nd, nr),
        out_shape=jax.ShapeDtypeStruct((nd, 2, tall, local + SUB, width), jnp.float32),
        in_specs=[whole],
        out_specs=whole,
        scratch_shapes=[sems] * 6,
        compiler_params=pltpu.CompilerParams(collective_id=0, has_side_effects=True),
        name="send",
    )(packed)
    return pl.pallas_call(
        functools.partial(link_kernel, nd, nr),
        out_shape=jax.ShapeDtypeStruct((2, dates, rows, width), jnp.float32),
        in_specs=[whole] * 3,
        out_specs=whole,
        scratch_shapes=[
            pltpu.VMEM((2, tall, dates + SUB, width), jnp.float32),
            pltpu.VMEM((nd, 2, tall, 2 * SUB, width), jnp.float32),
            pltpu.VMEM((nd, maps, width), jnp.bfloat16),
            pltpu.VMEM((nd, maps, width), jnp.bfloat16),
            pltpu.VMEM((local // SUB, 2 * width, width), jnp.bfloat16),
            pltpu.VMEM((rows, dates + SUB, width), jnp.float32),
            pltpu.VMEM((3, band, dates * rows, width), jnp.float32),
            pltpu.VMEM((2, 2, dates + band, rows, width), jnp.float32),
            pltpu.VMEM((dates, band), jnp.float32),
        ],
        compiler_params=pltpu.CompilerParams(vmem_limit_bytes=48 * 1024 * 1024),
        name="link",
    )(packed, landed, network.T)


def solution(mesh):
    return jax.shard_map(
        functools.partial(on_device, mesh.shape["date"], mesh.shape["row"]),
        mesh=mesh,
        in_specs=(P(None, "date", "row", None), P()),
        out_specs=P(None, None, "row", "date"),
        check_vma=False,
    )
```

```python
import functools

import jax
import jax.numpy as jnp
from jax import lax
from jax.experimental import pallas as pl
from jax.experimental.pallas import tpu as pltpu
from jax.sharding import PartitionSpec as P

LOOK = 5
ITERS = 5
SUB = 8
STEP = 16
MESH = pl.DeviceIdType.MESH


def pack_kernel(nd, x_ref, s_ref):
    _, dates, rows, cols = x_ref.shape
    width = cols // nd
    groups = dates // SUB
    slot = width // groups
    lane = lax.broadcasted_iota(jnp.int32, (rows, SUB, width), 2)
    for comp in range(2):
        rims = [jnp.zeros((rows, SUB, width), jnp.float32) for _ in range(nd)]
        for g in range(groups):
            near = pl.ds(g * SUB, SUB)
            tiles = []
            for c in range(nd):
                tile = x_ref[comp, near, :, pl.ds(c * width, width)]
                tile = jnp.transpose(tile, (1, 0, 2))
                s_ref[c, comp, :, near, :] = tile
                tiles.append(tile)
            first = slot * g
            for c in range(nd):
                if c > 0:
                    moved = pltpu.roll(tiles[c - 1], (first + LOOK) % width, 2)
                    rims[c] = jnp.where((lane >= first) & (lane < first + LOOK), moved, rims[c])
                if c < nd - 1:
                    moved = pltpu.roll(tiles[c + 1], (first + LOOK) % width, 2)
                    rims[c] = jnp.where((lane >= first + LOOK) & (lane < first + 2 * LOOK), moved, rims[c])
        for c in range(nd):
            s_ref[c, comp, :, pl.ds(dates, SUB), :] = rims[c]


def send_kernel(nd, nr, s_ref, e_ref, give_sem, take_sem, up_send, up_recv, down_send, down_recv):
    rows, deep = s_ref.shape[2:4]
    parts = give_sem.shape[1] // 2
    piece = deep // parts
    chunks = [(comp, part) for comp in range(2) for part in range(parts)]
    me = lax.axis_index("date")
    row = lax.axis_index("row")
    has_up = row > 0
    has_down = row < nr - 1
    up = jnp.maximum(row - 1, 0)
    down = jnp.minimum(row + 1, nr - 1)
    barrier = pltpu.get_barrier_semaphore()
    for k in range(1, nd):
        pl.semaphore_signal(barrier, 1, device_id=(lax.rem(me + k, nd), row), device_id_type=MESH)

    @pl.when(has_up)
    def _():
        pl.semaphore_signal(barrier, 1, device_id=(me, up), device_id_type=MESH)

    @pl.when(has_down)
    def _():
        pl.semaphore_signal(barrier, 1, device_id=(me, down), device_id_type=MESH)

    pl.semaphore_wait(barrier, nd - 1 + has_up.astype(jnp.int32) + has_down.astype(jnp.int32))

    def give(k, n):
        comp, part = chunks[n]
        there = lax.rem(me + k, nd)
        near = pl.ds(part * piece, piece)
        return pltpu.make_async_remote_copy(
            src_ref=s_ref.at[there, comp, :, near],
            dst_ref=e_ref.at[me, comp, pl.ds(LOOK, rows), near],
            send_sem=give_sem.at[k, n],
            recv_sem=take_sem.at[k, n],
            device_id=(there, row),
            device_id_type=MESH,
        )

    def rim(k, n, to_up):
        comp, part = chunks[n]
        near = pl.ds(part * piece, piece)
        source = lax.rem(me + nd - k, nd)
        begin = 0 if to_up else rows - LOOK
        if k == 0:
            src = s_ref.at[me, comp, pl.ds(begin, LOOK), near]
        else:
            src = e_ref.at[source, comp, pl.ds(LOOK + begin, LOOK), near]
        return pltpu.make_async_remote_copy(
            src_ref=src,
            dst_ref=e_ref.at[source, comp, pl.ds(LOOK + rows if to_up else 0, LOOK), near],
            send_sem=(up_send if to_up else down_send).at[k, n],
            recv_sem=(up_recv if to_up else down_recv).at[k, n],
            device_id=(me, up if to_up else down),
            device_id_type=MESH,
        )

    def start_rims(k, n):
        @pl.when(has_up)
        def _():
            rim(k, n, True).start()

        @pl.when(has_down)
        def _():
            rim(k, n, False).start()

    for n in range(len(chunks)):
        for k in range(1, nd):
            give(k, n).start()
        start_rims(0, n)
    for n in range(len(chunks)):
        for k in range(1, nd):
            give(k, n).wait_recv()
            start_rims(k, n)
    for n in range(len(chunks)):
        for k in range(1, nd):
            give(k, n).wait_send()
    for n in range(len(chunks)):
        for k in range(nd):

            @pl.when(has_up)
            def _():
                rim(k, n, True).wait_send()
                rim(k, n, False).wait_recv()

            @pl.when(has_down)
            def _():
                rim(k, n, False).wait_send()
                rim(k, n, True).wait_recv()


def row_sums(cells):
    span = 2 * LOOK + 1
    count = len(cells) - span + 1
    head = functools.reduce(jnp.add, cells[count - 1 : span])
    heads = [head]
    for k in range(count - 2, -1, -1):
        heads.append(heads[-1] + cells[k])
    heads = heads[::-1]
    sums = [heads[0]]
    tail = None
    for k in range(1, count):
        cell = cells[span + k - 1]
        tail = cell if tail is None else tail + cell
        sums.append(heads[k] + tail)
    return sums


def halves(sums):
    stacked = jnp.concatenate(sums, axis=0)
    high = stacked.astype(jnp.bfloat16)
    low = (stacked - high.astype(jnp.float32)).astype(jnp.bfloat16)
    return high, low


def products(load, offset):
    depth = load.rows
    if offset == 0:
        squares = []
        for r in range(depth):
            re, im = load(0, r, 0), load(1, r, 0)
            squares.append(re * re + im * im)
        return row_sums(squares)
    part_re, part_im = [], []
    for r in range(depth):
        a_re, a_im = load(0, r, 0), load(1, r, 0)
        b_re, b_im = load(0, r, offset), load(1, r, offset)
        part_re.append(a_re * b_re + a_im * b_im)
        part_im.append(a_im * b_re - a_re * b_im)
    return row_sums(part_re) + row_sums(part_im)


class Loader:
    def __init__(self, read, rows):
        self.read = read
        self.rows = rows

    def __call__(self, comp, row, offset):
        return self.read(comp, row, offset)


def link_kernel(nd, nr, s_ref, e_ref, net_ref, out_ref, main, rim, rim_high, rim_low, table, root, gam, vec, used_at):
    rows, width = out_ref.shape[2], out_ref.shape[3]
    dates = out_ref.shape[1]
    band = net_ref.shape[0]
    local = dates // nd
    groups = local // SUB
    slot = width // groups
    tiles = dates // SUB
    tall = rows + 2 * LOOK
    me = lax.axis_index("date")
    row = lax.axis_index("row")
    has_up = row > 0
    has_down = row < nr - 1

    used_at[...] = jnp.transpose(net_ref[...].astype(jnp.float32), (1, 0))

    lane = lax.broadcasted_iota(jnp.int32, (SUB, width), 1)
    for comp in range(2):
        for r in range(tall):
            inner = LOOK <= r < LOOK + rows
            keep = None if inner else (has_up if r < LOOK else has_down)
            for s in range(nd):
                block = e_ref[s, comp, r, pl.ds(0, local), :]
                edge = e_ref[s, comp, r, pl.ds(local, SUB), :]
                if keep is not None:
                    block = jnp.where(keep, block, 0.0)
                    edge = jnp.where(keep, edge, 0.0)
                main[comp, r, pl.ds(s * local, local), :] = block
                rim[s, comp, r, pl.ds(0, SUB), :] = edge
            if inner:
                main[comp, r, pl.ds(pl.multiple_of(me * local, SUB), local), :] = s_ref[me, comp, r - LOOK, pl.ds(0, local), :]
                rim[me, comp, r, pl.ds(0, SUB), :] = s_ref[me, comp, r - LOOK, pl.ds(local, SUB), :]
            main[comp, r, pl.ds(dates, SUB), :] = jnp.zeros((SUB, width), jnp.float32)
            for s in range(nd):
                later = pltpu.roll(rim[s, comp, r, pl.ds(0, SUB), :], width - slot, 1)
                if s + 1 < nd:
                    last = pltpu.roll(rim[s + 1, comp, r, pl.ds(0, SUB), :], slot * (groups - 1), 1)
                else:
                    last = jnp.zeros((SUB, width), jnp.float32)
                rim[s, comp, r, pl.ds(SUB, SUB), :] = jnp.where(lane >= slot * (groups - 1), last, later)

    inner = lax.broadcasted_iota(jnp.int32, (width, width), 0)
    outer = lax.broadcasted_iota(jnp.int32, (width, width), 1)
    for g in range(groups):
        table[g, pl.ds(0, width), :] = (jnp.abs(inner - outer) <= LOOK).astype(jnp.float32).astype(jnp.bfloat16)
        cell = inner - slot * g
        left = (cell >= 0) & (cell < LOOK) & (outer <= cell)
        right = (cell >= LOOK) & (cell < 2 * LOOK) & (outer >= width + cell - 2 * LOOK)
        table[g, pl.ds(width, width), :] = (left | right).astype(jnp.float32).astype(jnp.bfloat16)

    def rim_sums(s, carry):
        load = Loader(lambda comp, r, off: rim[s, comp, r, pl.ds(off, SUB), :], tall)
        begin = 0
        for offset in range(band + 1):
            high, low = halves(products(load, offset))
            rim_high[s, pl.ds(begin, high.shape[0]), :] = high
            rim_low[s, pl.ds(begin, high.shape[0]), :] = low
            begin += high.shape[0]
        return carry

    lax.fori_loop(0, nd, rim_sums, 0)

    for k in range(rows):
        root[k, pl.ds(dates, SUB), :] = jnp.zeros((SUB, width), jnp.float32)

    def tile_sums(index, carry):
        t = tiles - 1 - index
        s, g = t // groups, lax.rem(t, groups)
        base = t * SUB
        load = Loader(lambda comp, r, off: main[comp, r, pl.ds(base + off, SUB), :], tall)
        used = used_at[pl.ds(base, SUB), :]
        begin = 0
        for offset in range(band + 1):
            high, low = halves(products(load, offset))
            count = high.shape[0]
            high = jnp.concatenate([high, rim_high[s, pl.ds(begin, count), :]], axis=1)
            low = jnp.concatenate([low, rim_low[s, pl.ds(begin, count), :]], axis=1)
            begin += count
            sums = jnp.dot(jnp.concatenate([high, low], axis=0), table[g], preferred_element_type=jnp.float32)
            sums = sums[:count] + sums[count:]
            for k in range(rows):
                if offset == 0:
                    root[k, pl.ds(base, SUB), :] = lax.rsqrt(sums[k * SUB : (k + 1) * SUB] + 1e-06)
                else:
                    weight = root[k, pl.ds(base, SUB), :] * root[k, pl.ds(base + offset, SUB), :]
                    weight = weight * used[:, offset - 1 : offset]
                    at = pl.ds(base * rows + k, SUB, stride=rows)
                    c_re = sums[k * SUB : (k + 1) * SUB] * weight
                    c_im = sums[(rows + k) * SUB : (rows + k + 1) * SUB] * weight
                    gam[0, offset - 1, at, :] = c_re
                    gam[1, offset - 1, at, :] = c_re + c_im
                    gam[2, offset - 1, at, :] = c_im - c_re
        return carry

    lax.fori_loop(0, tiles, tile_sums, 0)

    zero = jnp.zeros((rows, width), jnp.float32)
    for buf in range(2):
        for comp in range(2):
            for d in range(band):
                vec[buf, comp, dates + d] = zero

    def at_date(d):
        return pl.ds(pl.multiple_of(d * rows, rows), rows)

    def first(b, carry):
        back_re, back_sum, total = list(carry[0]), list(carry[1]), carry[2]
        for j in range(SUB):
            d = b * SUB + j
            y_re = back_re[j] + 1.0
            y_im = back_re[j] - back_sum[j]
            ahead_re = ahead_sum = None
            for o in range(1, band + 1):
                c_re = gam[0, o - 1, at_date(d), :]
                c_sum = gam[1, o - 1, at_date(d), :]
                ahead_re = c_re if ahead_re is None else ahead_re + c_re
                ahead_sum = c_sum if ahead_sum is None else ahead_sum + c_sum
                if o == band:
                    back_re.append(c_re)
                    back_sum.append(c_sum)
                else:
                    back_re[j + o] = back_re[j + o] + c_re
                    back_sum[j + o] = back_sum[j + o] + c_sum
            y_re = y_re + ahead_re
            y_im = y_im + (ahead_sum - ahead_re)
            vec[1, 0, d] = y_re
            vec[1, 1, d] = y_im
            total = total + (y_re * y_re + y_im * y_im)
        return tuple(back_re[SUB:]), tuple(back_sum[SUB:]), total

    none = tuple(zero for _ in range(band))
    _, _, total = lax.fori_loop(0, tiles, first, (none, none, zero))
    scale = lax.rsqrt(total / dates + 1e-06)

    def iterate(step, scale):
        now = lax.rem(step, 2)
        after = 1 - now

        def block(b, carry):
            acc, near, total = carry
            acc_a, acc_b, acc_c = [list(a) for a in acc]
            v_re, v_im, v_sum = [list(a) for a in near]
            for j in range(STEP):
                d = b * STEP + j
                v_re.append(vec[now, 0, d + band])
                v_im.append(vec[now, 1, d + band])
                v_sum.append(v_re[-1] + v_im[-1])
                y_a, y_b, y_c = acc_a[j], -acc_b[j], -acc_c[j]
                for o in range(1, band + 1):
                    c_re = gam[0, o - 1, at_date(d), :]
                    c_sum = gam[1, o - 1, at_date(d), :]
                    c_dif = gam[2, o - 1, at_date(d), :]
                    y_a = y_a + c_re * v_sum[j + o]
                    y_b = y_b + c_dif * v_re[j + o]
                    y_c = y_c + c_sum * v_im[j + o]
                    back_a = c_re * v_sum[j]
                    back_b = c_sum * v_re[j]
                    back_c = c_dif * v_im[j]
                    if o == band:
                        acc_a.append(back_a)
                        acc_b.append(back_b)
                        acc_c.append(back_c)
                    else:
                        acc_a[j + o] = acc_a[j + o] + back_a
                        acc_b[j + o] = acc_b[j + o] + back_b
                        acc_c[j + o] = acc_c[j + o] + back_c
                y_re = v_re[j] + (y_a - y_c)
                y_im = v_im[j] + (y_a + y_b)
                vec[after, 0, d] = y_re
                vec[after, 1, d] = y_im
                total = total + (y_re * y_re + y_im * y_im)
            acc = tuple(acc_a[STEP:]), tuple(acc_b[STEP:]), tuple(acc_c[STEP:])
            near = tuple(v_re[STEP:]), tuple(v_im[STEP:]), tuple(v_sum[STEP:])
            return acc, near, total

        v_re = tuple(vec[now, 0, d] for d in range(band))
        v_im = tuple(vec[now, 1, d] for d in range(band))
        v_sum = tuple(a + b for a, b in zip(v_re, v_im))
        _, _, total = lax.fori_loop(0, dates // STEP, block, ((none, none, none), (v_re, v_im, v_sum), zero))
        return scale * lax.rsqrt(scale * scale * (total / dates) + 1e-06)

    scale = lax.fori_loop(1, ITERS, iterate, scale)
    final = ITERS % 2

    def finish(b, carry):
        for j in range(SUB):
            d = b * SUB + j
            out_ref[0, d] = vec[final, 0, d] * scale
            out_ref[1, d] = vec[final, 1, d] * scale
        return carry

    lax.fori_loop(0, tiles, finish, 0)


def on_device(nd, nr, slc, network):
    _, local, rows, cols = slc.shape
    width = cols // nd
    dates, band = network.shape
    tall = rows + 2 * LOOK
    maps = (2 * band + 1) * rows * SUB
    whole = pl.BlockSpec(memory_space=pltpu.VMEM)
    away = pl.BlockSpec(memory_space=pl.ANY)
    packed = pl.pallas_call(
        functools.partial(pack_kernel, nd),
        out_shape=jax.ShapeDtypeStruct((nd, 2, rows, local + SUB, width), jnp.float32),
        in_specs=[whole],
        out_specs=whole,
        name="pack",
    )(slc)
    parts = 3 if (local + SUB) % (3 * SUB) == 0 else 1
    sems = pltpu.SemaphoreType.DMA((nd, 2 * parts))
    landed = pl.pallas_call(
        functools.partial(send_kernel, nd, nr),
        out_shape=jax.ShapeDtypeStruct((nd, 2, tall, local + SUB, width), jnp.float32),
        in_specs=[away],
        out_specs=away,
        scratch_shapes=[sems] * 6,
        compiler_params=pltpu.CompilerParams(collective_id=0, has_side_effects=True),
        name="send",
    )(packed)
    return pl.pallas_call(
        functools.partial(link_kernel, nd, nr),
        out_shape=jax.ShapeDtypeStruct((2, dates, rows, width), jnp.float32),
        in_specs=[whole] * 3,
        out_specs=whole,
        scratch_shapes=[
            pltpu.VMEM((2, tall, dates + SUB, width), jnp.float32),
            pltpu.VMEM((nd, 2, tall, 2 * SUB, width), jnp.float32),
            pltpu.VMEM((nd, maps, width), jnp.bfloat16),
            pltpu.VMEM((nd, maps, width), jnp.bfloat16),
            pltpu.VMEM((local // SUB, 2 * width, width), jnp.bfloat16),
            pltpu.VMEM((rows, dates + SUB, width), jnp.float32),
            pltpu.VMEM((3, band, dates * rows, width), jnp.float32),
            pltpu.VMEM((2, 2, dates + band, rows, width), jnp.float32),
            pltpu.VMEM((dates, band), jnp.float32),
        ],
        compiler_params=pltpu.CompilerParams(vmem_limit_bytes=48 * 1024 * 1024),
        name="link",
    )(packed, landed, network.T)


def solution(mesh):
    return jax.shard_map(
        functools.partial(on_device, mesh.shape["date"], mesh.shape["row"]),
        mesh=mesh,
        in_specs=(P(None, "date", "row", None), P()),
        out_specs=P(None, None, "row", "date"),
        check_vma=False,
    )
```

```python
import functools

import jax
import jax.numpy as jnp
from jax import lax
from jax.experimental import pallas as pl
from jax.experimental.pallas import tpu as pltpu
from jax.sharding import PartitionSpec as P

LOOK = 5
ITERS = 5
SUB = 8
STEP = 16
MESH = pl.DeviceIdType.MESH


def pack_kernel(nd, x_ref, s_ref):
    _, dates, rows, cols = x_ref.shape
    width = cols // nd
    groups = dates // SUB
    slot = width // groups
    lane = lax.broadcasted_iota(jnp.int32, (rows, SUB, width), 2)
    for comp in range(2):
        rims = [jnp.zeros((rows, SUB, width), jnp.float32) for _ in range(nd)]
        for g in range(groups):
            near = pl.ds(g * SUB, SUB)
            tiles = []
            for c in range(nd):
                tile = x_ref[comp, near, :, pl.ds(c * width, width)]
                tile = jnp.transpose(tile, (1, 0, 2))
                s_ref[c, comp, :, near, :] = tile
                tiles.append(tile)
            first = slot * g
            for c in range(nd):
                if c > 0:
                    moved = pltpu.roll(tiles[c - 1], (first + LOOK) % width, 2)
                    rims[c] = jnp.where((lane >= first) & (lane < first + LOOK), moved, rims[c])
                if c < nd - 1:
                    moved = pltpu.roll(tiles[c + 1], (first + LOOK) % width, 2)
                    rims[c] = jnp.where((lane >= first + LOOK) & (lane < first + 2 * LOOK), moved, rims[c])
        for c in range(nd):
            s_ref[c, comp, :, pl.ds(dates, SUB), :] = rims[c]


def send_kernel(nd, nr, s_ref, e_ref, give_sem, take_sem, up_send, up_recv, down_send, down_recv):
    rows, deep = s_ref.shape[2:4]
    parts = give_sem.shape[1] // 2
    piece = deep // parts
    chunks = [(comp, part) for comp in range(2) for part in range(parts)]
    me = lax.axis_index("date")
    row = lax.axis_index("row")
    has_up = row > 0
    has_down = row < nr - 1
    up = jnp.maximum(row - 1, 0)
    down = jnp.minimum(row + 1, nr - 1)
    barrier = pltpu.get_barrier_semaphore()
    for k in range(1, nd):
        pl.semaphore_signal(barrier, 1, device_id=(lax.rem(me + k, nd), row), device_id_type=MESH)

    @pl.when(has_up)
    def _():
        pl.semaphore_signal(barrier, 1, device_id=(me, up), device_id_type=MESH)

    @pl.when(has_down)
    def _():
        pl.semaphore_signal(barrier, 1, device_id=(me, down), device_id_type=MESH)

    pl.semaphore_wait(barrier, nd - 1 + has_up.astype(jnp.int32) + has_down.astype(jnp.int32))

    def give(k, n):
        comp, part = chunks[n]
        there = lax.rem(me + k, nd)
        near = pl.ds(part * piece, piece)
        return pltpu.make_async_remote_copy(
            src_ref=s_ref.at[there, comp, :, near],
            dst_ref=e_ref.at[me, comp, pl.ds(LOOK, rows), near],
            send_sem=give_sem.at[k, n],
            recv_sem=take_sem.at[k, n],
            device_id=(there, row),
            device_id_type=MESH,
        )

    def rim(k, n, to_up):
        comp, part = chunks[n]
        near = pl.ds(part * piece, piece)
        source = lax.rem(me + nd - k, nd)
        begin = 0 if to_up else rows - LOOK
        if k == 0:
            src = s_ref.at[me, comp, pl.ds(begin, LOOK), near]
        else:
            src = e_ref.at[source, comp, pl.ds(LOOK + begin, LOOK), near]
        return pltpu.make_async_remote_copy(
            src_ref=src,
            dst_ref=e_ref.at[source, comp, pl.ds(LOOK + rows if to_up else 0, LOOK), near],
            send_sem=(up_send if to_up else down_send).at[k, n],
            recv_sem=(up_recv if to_up else down_recv).at[k, n],
            device_id=(me, up if to_up else down),
            device_id_type=MESH,
        )

    def start_rims(k, n):
        @pl.when(has_up)
        def _():
            rim(k, n, True).start()

        @pl.when(has_down)
        def _():
            rim(k, n, False).start()

    for n in range(len(chunks)):
        for k in range(1, nd):
            give(k, n).start()
        start_rims(0, n)
    for n in range(len(chunks)):
        for k in range(1, nd):
            give(k, n).wait_recv()
            start_rims(k, n)
    for n in range(len(chunks)):
        for k in range(1, nd):
            give(k, n).wait_send()
    for n in range(len(chunks)):
        for k in range(nd):

            @pl.when(has_up)
            def _():
                rim(k, n, True).wait_send()
                rim(k, n, False).wait_recv()

            @pl.when(has_down)
            def _():
                rim(k, n, False).wait_send()
                rim(k, n, True).wait_recv()


def row_sums(cells):
    span = 2 * LOOK + 1
    count = len(cells) - span + 1
    head = functools.reduce(jnp.add, cells[count - 1 : span])
    heads = [head]
    for k in range(count - 2, -1, -1):
        heads.append(heads[-1] + cells[k])
    heads = heads[::-1]
    sums = [heads[0]]
    tail = None
    for k in range(1, count):
        cell = cells[span + k - 1]
        tail = cell if tail is None else tail + cell
        sums.append(heads[k] + tail)
    return sums


def halves(sums):
    stacked = jnp.concatenate(sums, axis=0)
    high = stacked.astype(jnp.bfloat16)
    low = (stacked - high.astype(jnp.float32)).astype(jnp.bfloat16)
    return high, low


def products(load, offset):
    depth = load.rows
    if offset == 0:
        squares = []
        for r in range(depth):
            re, im = load(0, r, 0), load(1, r, 0)
            squares.append(re * re + im * im)
        return row_sums(squares)
    part_re, part_im = [], []
    for r in range(depth):
        a_re, a_im = load(0, r, 0), load(1, r, 0)
        b_re, b_im = load(0, r, offset), load(1, r, offset)
        part_re.append(a_re * b_re + a_im * b_im)
        part_im.append(a_im * b_re - a_re * b_im)
    return row_sums(part_re) + row_sums(part_im)


class Loader:
    def __init__(self, read, rows):
        self.read = read
        self.rows = rows

    def __call__(self, comp, row, offset):
        return self.read(comp, row, offset)


def link_kernel(nd, nr, s_ref, e_ref, net_ref, out_ref, main, rim, rim_high, rim_low, table, root, gam, vec, used_at):
    rows, width = out_ref.shape[2], out_ref.shape[3]
    dates = out_ref.shape[1]
    band = net_ref.shape[0]
    local = dates // nd
    groups = local // SUB
    slot = width // groups
    tiles = dates // SUB
    tall = rows + 2 * LOOK
    me = lax.axis_index("date")
    row = lax.axis_index("row")
    has_up = row > 0
    has_down = row < nr - 1

    used_at[...] = jnp.transpose(net_ref[...].astype(jnp.float32), (1, 0))

    lane = lax.broadcasted_iota(jnp.int32, (SUB, width), 1)
    for comp in range(2):
        for r in range(tall):
            inner = LOOK <= r < LOOK + rows
            keep = None if inner else (has_up if r < LOOK else has_down)
            for s in range(nd):
                block = e_ref[s, comp, r, pl.ds(0, local), :]
                edge = e_ref[s, comp, r, pl.ds(local, SUB), :]
                if keep is not None:
                    block = jnp.where(keep, block, 0.0)
                    edge = jnp.where(keep, edge, 0.0)
                main[comp, r, pl.ds(s * local, local), :] = block
                rim[s, comp, r, pl.ds(0, SUB), :] = edge
            if inner:
                main[comp, r, pl.ds(pl.multiple_of(me * local, SUB), local), :] = s_ref[me, comp, r - LOOK, pl.ds(0, local), :]
                rim[me, comp, r, pl.ds(0, SUB), :] = s_ref[me, comp, r - LOOK, pl.ds(local, SUB), :]
            main[comp, r, pl.ds(dates, SUB), :] = jnp.zeros((SUB, width), jnp.float32)
            for s in range(nd):
                later = pltpu.roll(rim[s, comp, r, pl.ds(0, SUB), :], width - slot, 1)
                if s + 1 < nd:
                    last = pltpu.roll(rim[s + 1, comp, r, pl.ds(0, SUB), :], slot * (groups - 1), 1)
                else:
                    last = jnp.zeros((SUB, width), jnp.float32)
                rim[s, comp, r, pl.ds(SUB, SUB), :] = jnp.where(lane >= slot * (groups - 1), last, later)

    inner = lax.broadcasted_iota(jnp.int32, (width, width), 0)
    outer = lax.broadcasted_iota(jnp.int32, (width, width), 1)
    for g in range(groups):
        table[g, pl.ds(0, width), :] = (jnp.abs(inner - outer) <= LOOK).astype(jnp.float32).astype(jnp.bfloat16)
        cell = inner - slot * g
        left = (cell >= 0) & (cell < LOOK) & (outer <= cell)
        right = (cell >= LOOK) & (cell < 2 * LOOK) & (outer >= width + cell - 2 * LOOK)
        table[g, pl.ds(width, width), :] = (left | right).astype(jnp.float32).astype(jnp.bfloat16)

    def rim_sums(s, carry):
        load = Loader(lambda comp, r, off: rim[s, comp, r, pl.ds(off, SUB), :], tall)
        begin = 0
        for offset in range(band + 1):
            high, low = halves(products(load, offset))
            rim_high[s, pl.ds(begin, high.shape[0]), :] = high
            rim_low[s, pl.ds(begin, high.shape[0]), :] = low
            begin += high.shape[0]
        return carry

    lax.fori_loop(0, nd, rim_sums, 0)

    for k in range(rows):
        root[k, pl.ds(dates, SUB), :] = jnp.zeros((SUB, width), jnp.float32)

    def tile_sums(index, carry):
        t = tiles - 1 - index
        s, g = t // groups, lax.rem(t, groups)
        base = t * SUB
        load = Loader(lambda comp, r, off: main[comp, r, pl.ds(base + off, SUB), :], tall)
        used = used_at[pl.ds(base, SUB), :]
        begin = 0
        for offset in range(band + 1):
            high, low = halves(products(load, offset))
            count = high.shape[0]
            high = jnp.concatenate([high, rim_high[s, pl.ds(begin, count), :]], axis=1)
            low = jnp.concatenate([low, rim_low[s, pl.ds(begin, count), :]], axis=1)
            begin += count
            sums = jnp.dot(high, table[g], preferred_element_type=jnp.float32)
            sums = sums + jnp.dot(low, table[g], preferred_element_type=jnp.float32)
            for k in range(rows):
                if offset == 0:
                    root[k, pl.ds(base, SUB), :] = lax.rsqrt(sums[k * SUB : (k + 1) * SUB] + 1e-06)
                else:
                    weight = root[k, pl.ds(base, SUB), :] * root[k, pl.ds(base + offset, SUB), :]
                    weight = weight * used[:, offset - 1 : offset]
                    at = pl.ds(base * rows + k, SUB, stride=rows)
                    c_re = sums[k * SUB : (k + 1) * SUB] * weight
                    c_im = sums[(rows + k) * SUB : (rows + k + 1) * SUB] * weight
                    gam[0, offset - 1, at, :] = c_re
                    gam[1, offset - 1, at, :] = c_re + c_im
                    gam[2, offset - 1, at, :] = c_im - c_re
        return carry

    lax.fori_loop(0, tiles, tile_sums, 0)

    zero = jnp.zeros((rows, width), jnp.float32)
    for buf in range(2):
        for comp in range(2):
            for d in range(band):
                vec[buf, comp, dates + d] = zero

    def at_date(d):
        return pl.ds(pl.multiple_of(d * rows, rows), rows)

    def first(b, carry):
        back_re, back_sum, total = list(carry[0]), list(carry[1]), carry[2]
        for j in range(SUB):
            d = b * SUB + j
            y_re = back_re[j] + 1.0
            y_im = back_re[j] - back_sum[j]
            ahead_re = ahead_sum = None
            for o in range(1, band + 1):
                c_re = gam[0, o - 1, at_date(d), :]
                c_sum = gam[1, o - 1, at_date(d), :]
                ahead_re = c_re if ahead_re is None else ahead_re + c_re
                ahead_sum = c_sum if ahead_sum is None else ahead_sum + c_sum
                if o == band:
                    back_re.append(c_re)
                    back_sum.append(c_sum)
                else:
                    back_re[j + o] = back_re[j + o] + c_re
                    back_sum[j + o] = back_sum[j + o] + c_sum
            y_re = y_re + ahead_re
            y_im = y_im + (ahead_sum - ahead_re)
            vec[1, 0, d] = y_re
            vec[1, 1, d] = y_im
            total = total + (y_re * y_re + y_im * y_im)
        return tuple(back_re[SUB:]), tuple(back_sum[SUB:]), total

    none = tuple(zero for _ in range(band))
    _, _, total = lax.fori_loop(0, tiles, first, (none, none, zero))
    scale = lax.rsqrt(total / dates + 1e-06)

    def iterate(step, scale):
        now = lax.rem(step, 2)
        after = 1 - now

        def block(b, carry):
            acc, near, total = carry
            acc_a, acc_b, acc_c = [list(a) for a in acc]
            v_re, v_im, v_sum = [list(a) for a in near]
            for j in range(STEP):
                d = b * STEP + j
                v_re.append(vec[now, 0, d + band])
                v_im.append(vec[now, 1, d + band])
                v_sum.append(v_re[-1] + v_im[-1])
                y_a, y_b, y_c = acc_a[j], -acc_b[j], -acc_c[j]
                for o in range(1, band + 1):
                    c_re = gam[0, o - 1, at_date(d), :]
                    c_sum = gam[1, o - 1, at_date(d), :]
                    c_dif = gam[2, o - 1, at_date(d), :]
                    y_a = y_a + c_re * v_sum[j + o]
                    y_b = y_b + c_dif * v_re[j + o]
                    y_c = y_c + c_sum * v_im[j + o]
                    back_a = c_re * v_sum[j]
                    back_b = c_sum * v_re[j]
                    back_c = c_dif * v_im[j]
                    if o == band:
                        acc_a.append(back_a)
                        acc_b.append(back_b)
                        acc_c.append(back_c)
                    else:
                        acc_a[j + o] = acc_a[j + o] + back_a
                        acc_b[j + o] = acc_b[j + o] + back_b
                        acc_c[j + o] = acc_c[j + o] + back_c
                y_re = v_re[j] + (y_a - y_c)
                y_im = v_im[j] + (y_a + y_b)
                vec[after, 0, d] = y_re
                vec[after, 1, d] = y_im
                total = total + (y_re * y_re + y_im * y_im)
            acc = tuple(acc_a[STEP:]), tuple(acc_b[STEP:]), tuple(acc_c[STEP:])
            near = tuple(v_re[STEP:]), tuple(v_im[STEP:]), tuple(v_sum[STEP:])
            return acc, near, total

        v_re = tuple(vec[now, 0, d] for d in range(band))
        v_im = tuple(vec[now, 1, d] for d in range(band))
        v_sum = tuple(a + b for a, b in zip(v_re, v_im))
        _, _, total = lax.fori_loop(0, dates // STEP, block, ((none, none, none), (v_re, v_im, v_sum), zero))
        return scale * lax.rsqrt(scale * scale * (total / dates) + 1e-06)

    scale = lax.fori_loop(1, ITERS, iterate, scale)
    final = ITERS % 2

    def finish(b, carry):
        for j in range(SUB):
            d = b * SUB + j
            out_ref[0, d] = vec[final, 0, d] * scale
            out_ref[1, d] = vec[final, 1, d] * scale
        return carry

    lax.fori_loop(0, tiles, finish, 0)


def on_device(nd, nr, slc, network):
    _, local, rows, cols = slc.shape
    width = cols // nd
    dates, band = network.shape
    tall = rows + 2 * LOOK
    maps = (2 * band + 1) * rows * SUB
    whole = pl.BlockSpec(memory_space=pltpu.VMEM)
    away = pl.BlockSpec(memory_space=pl.ANY)
    packed = pl.pallas_call(
        functools.partial(pack_kernel, nd),
        out_shape=jax.ShapeDtypeStruct((nd, 2, rows, local + SUB, width), jnp.float32),
        in_specs=[whole],
        out_specs=whole,
        name="pack",
    )(slc)
    parts = (local + SUB) // SUB
    sems = pltpu.SemaphoreType.DMA((nd, 2 * parts))
    landed = pl.pallas_call(
        functools.partial(send_kernel, nd, nr),
        out_shape=jax.ShapeDtypeStruct((nd, 2, tall, local + SUB, width), jnp.float32),
        in_specs=[away],
        out_specs=away,
        scratch_shapes=[sems] * 6,
        compiler_params=pltpu.CompilerParams(collective_id=0, has_side_effects=True),
        name="send",
    )(packed)
    return pl.pallas_call(
        functools.partial(link_kernel, nd, nr),
        out_shape=jax.ShapeDtypeStruct((2, dates, rows, width), jnp.float32),
        in_specs=[whole] * 3,
        out_specs=whole,
        scratch_shapes=[
            pltpu.VMEM((2, tall, dates + SUB, width), jnp.float32),
            pltpu.VMEM((nd, 2, tall, 2 * SUB, width), jnp.float32),
            pltpu.VMEM((nd, maps, width), jnp.bfloat16),
            pltpu.VMEM((nd, maps, width), jnp.bfloat16),
            pltpu.VMEM((local // SUB, 2 * width, width), jnp.bfloat16),
            pltpu.VMEM((rows, dates + SUB, width), jnp.float32),
            pltpu.VMEM((3, band, dates * rows, width), jnp.float32),
            pltpu.VMEM((2, 2, dates + band, rows, width), jnp.float32),
            pltpu.VMEM((dates, band), jnp.float32),
        ],
        compiler_params=pltpu.CompilerParams(vmem_limit_bytes=48 * 1024 * 1024),
        name="link",
    )(packed, landed, network.T)


def solution(mesh):
    return jax.shard_map(
        functools.partial(on_device, mesh.shape["date"], mesh.shape["row"]),
        mesh=mesh,
        in_specs=(P(None, "date", "row", None), P()),
        out_specs=P(None, None, "row", "date"),
        check_vma=False,
    )
```
